512 devices in a mesh: slab: 64 (over z, x), strip: 8 (over y, core).
Axes of the slice: x: 4, y: 4, z: 16, core: 2. Of those that a mesh axis runs over, the one named last changes fastest.
Arguments:
- query_rows: bfloat16 [512, 48, 4096], P('slab', 'strip'), may hold values from -8 to 8
- key_rows: bfloat16 [512, 48, 4096], P('slab', 'strip'), may hold values from -8 to 8
- value_rows: bfloat16 [512, 48, 4096], P('slab', 'strip'), may hold values from -6 to 6
- window_offsets: int32 [8, 3], replicated, may hold values from -1 to 1, as said below
Outputs:
- attended: bfloat16 [512, 48, 4096], P('slab', 'strip')
The draws below stay inside these ranges and needn't reach their ends.
Inputs may be any that keep to these rules, and one draw needn't show every extreme that they name: `window_offsets`: each row is a tile offset (dt, dh, dw); the 8 rows are distinct, one of them is (0, 0, 0), some row has dt = -1 and some row has dt = 1.
All inputs are finite; a program needn't handle non-finite values.
Results may differ from the reference program's by a relative error of at most 0.0049.
Values may be sent and summed in bfloat16 or wider, within the bound.
No kernel may reach another device: no remote copies, remote signals or barrier semaphores. Data moves between devices by JAX's collectives and lax.ppermute only.
A program may use at most 128 MiB of HBM per device.

```python
import jax
import jax.numpy as jnp
from jax import lax

HEADS = 32
HD = 128
TILE_T = 4
TILE_H = 8
TILE_W = 8
WIN = 8
HEIGHT = 16
WIDTH = 48
FRAMES = 32
LINES = 512


def draw_query_rows(key, part):
    line_count = FRAMES * HEIGHT
    full_shape = (line_count, WIDTH, HEADS * HD)
    return jnp.clip(jax.random.normal(jax.random.fold_in(key, 13), full_shape, jnp.float32), -8.0, 8.0).astype(jnp.bfloat16)


def draw_key_rows(key, part):
    line_count = FRAMES * HEIGHT
    full_shape = (line_count, WIDTH, HEADS * HD)
    return jnp.clip(jax.random.normal(jax.random.fold_in(key, 11), full_shape, jnp.float32), -8.0, 8.0).astype(jnp.bfloat16)


def draw_window_offsets(key, part):
    shuffled = jax.random.permutation(jax.random.fold_in(key, 21), 27)
    positions = jnp.argsort(shuffled, stable=True).astype(jnp.int32)
    code_list = jnp.arange(27, dtype=jnp.int32)
    early_minus = jnp.argmin(jnp.where(code_list < 9, positions, 99)).astype(jnp.int32)
    early_plus = jnp.argmin(jnp.where(code_list >= 18, positions, 99)).astype(jnp.int32)
    priority = positions + 100
    priority = jnp.where(code_list == 13, 0, priority)
    priority = jnp.where(code_list == early_minus, 1, priority)
    priority = jnp.where(code_list == early_plus, 2, priority)
    picked = jnp.argsort(priority, stable=True)[:WIN].astype(jnp.int32)
    picked = picked[jax.random.permutation(jax.random.fold_in(key, 23), WIN)]
    offset_rows = jnp.stack([picked // 9 - 1, picked // 3 % 3 - 1, picked % 3 - 1], axis=1)
    return offset_rows.astype(jnp.int32)


def steps_of(key, dims, split, low, high):
    loudness, own = 1.0, jax.random.fold_in(key, 6)
    for dim, shards_of in split:
        steps = jnp.exp(jax.random.uniform(jax.random.fold_in(own, dim), (shards_of,), jnp.float32, low / len(split), high / len(split)))
        loudness = loudness * jnp.repeat(steps, dims[dim] // shards_of).reshape([-1 if axis == dim else 1 for axis in range(len(dims))])
    return loudness


def scatter_about(stream_key, shape, scale, most, split=(), held_as=jnp.bfloat16):
    result = scale * jax.random.normal(stream_key, shape, jnp.float32)
    if split:
        result = result * steps_of(stream_key, shape, split, -0.22, 0.18)
    return jnp.clip(result, -most, most).astype(held_as)


def setup_inputs(seed: int = 0) -> dict:
    splits = jax.random.split(jax.random.key(seed), 5)
    query_rows = draw_query_rows(jax.random.fold_in(splits[4], 71), 0)
    key_rows = draw_key_rows(jax.random.fold_in(splits[4], 71), 0)
    value_rows = scatter_about(splits[2], (LINES, WIDTH, HEADS * HD), 1.0, 6.0, ((0, 64), (1, 8)))
    window_offsets = draw_window_offsets(jax.random.fold_in(splits[4], 71), 0)
    return dict(query_rows=query_rows, key_rows=key_rows, value_rows=value_rows, window_offsets=window_offsets)


def tile_major(field):
    shaped = field.reshape(FRAMES // TILE_T, TILE_T, HEIGHT // TILE_H, TILE_H, WIDTH // TILE_W, TILE_W, HEADS, HD)
    shaped = shaped.transpose(6, 0, 2, 4, 1, 3, 5, 7)
    return shaped.reshape(HEADS, FRAMES // TILE_T, HEIGHT // TILE_H, WIDTH // TILE_W, TILE_T * TILE_H * TILE_W, HD)


def reference(query_rows, key_rows, value_rows, window_offsets):
    frame_tiles = FRAMES // TILE_T
    row_tiles = HEIGHT // TILE_H
    col_tiles = WIDTH // TILE_W
    tokens = TILE_T * TILE_H * TILE_W
    padding = ((0, 0), (1, 1), (1, 1), (1, 1), (0, 0), (0, 0))
    query_tiles = tile_major(query_rows)
    key_tiles = jnp.pad(tile_major(key_rows), padding)
    value_tiles = jnp.pad(tile_major(value_rows), padding)
    grid_shape = (frame_tiles, row_tiles, col_tiles, WIN)
    key_frame = jnp.broadcast_to(jnp.arange(frame_tiles, dtype=jnp.int32)[:, None, None, None] + window_offsets[:, 0], grid_shape)
    key_row = jnp.broadcast_to(jnp.arange(row_tiles, dtype=jnp.int32)[None, :, None, None] + window_offsets[:, 1], grid_shape)
    key_col = jnp.broadcast_to(jnp.arange(col_tiles, dtype=jnp.int32)[None, None, :, None] + window_offsets[:, 2], grid_shape)
    inside = (key_frame >= 0) & (key_frame < frame_tiles) & (key_row >= 0) & (key_row < row_tiles)
    inside = inside & (key_col >= 0) & (key_col < col_tiles)
    score_scale = HD ** -0.5

    def one_head(tensors):
        query_head, key_head, value_head = tensors

        def one_layer(layer_index):
            query_layer = lax.dynamic_index_in_dim(query_head, layer_index, 0, keepdims=False).astype(jnp.float32)
            frame_pick = lax.dynamic_index_in_dim(key_frame, layer_index, 0, keepdims=False) + 1
            row_pick = lax.dynamic_index_in_dim(key_row, layer_index, 0, keepdims=False) + 1
            col_pick = lax.dynamic_index_in_dim(key_col, layer_index, 0, keepdims=False) + 1
            live_tiles = lax.dynamic_index_in_dim(inside, layer_index, 0, keepdims=False)
            window_keys = key_head[frame_pick, row_pick, col_pick].reshape(row_tiles, col_tiles, WIN * tokens, HD).astype(jnp.float32)
            window_values = value_head[frame_pick, row_pick, col_pick].reshape(row_tiles, col_tiles, WIN * tokens, HD).astype(jnp.float32)
            scores = jnp.einsum("hwqd,hwkd->hwqk", query_layer, window_keys) * score_scale
            key_live = jnp.repeat(live_tiles, tokens, axis=2)
            scores = jnp.where(key_live[:, :, None, :], scores, -1e30)
            row_max = jnp.max(scores, axis=-1, keepdims=True)
            raised = jnp.exp(scores - row_max)
            weights = (raised / jnp.sum(raised, axis=-1, keepdims=True)).astype(jnp.bfloat16)
            weights = lax.optimization_barrier(weights)
            mixed_out = jnp.einsum("hwqk,hwkd->hwqd", weights.astype(jnp.float32), window_values)
            return mixed_out.astype(jnp.bfloat16)

        return lax.map(one_layer, jnp.arange(frame_tiles, dtype=jnp.int32))

    attended = lax.map(one_head, (query_tiles, key_tiles, value_tiles))
    attended = attended.reshape(HEADS, frame_tiles, row_tiles, col_tiles, TILE_T, TILE_H, TILE_W, HD)
    attended = attended.transpose(1, 4, 2, 5, 3, 6, 0, 7)
    return attended.reshape(FRAMES * HEIGHT, WIDTH, HEADS * HD)
```

```python
import jax
import jax.numpy as jnp
from jax import lax
from jax.experimental import pallas as pl
from jax.experimental.pallas import tpu as pltpu
from jax.sharding import Mesh, PartitionSpec as P

HD = 128
HEADS = 32
STRIP = 6
ROWS = 8
PIECE = STRIP * ROWS
SPAN = 8 * PIECE
CHUNK = 64
TILE = 256
COLS = 6
WIN = 8
CHIPS = 32
C2 = HD ** (-0.5) * 1.4426950408889634
LOW = -1e30


def pack_body(count, *refs):
    ins, out_ref, flat = refs[:count], refs[count], refs[count + 1]
    row = lax.broadcasted_iota(jnp.int32, (PIECE, 64), 0)
    col = lax.broadcasted_iota(jnp.int32, (PIECE, 64), 1)
    perm = (col == (row % ROWS) * 8 + row // ROWS).astype(jnp.bfloat16)
    flat[...] = jnp.zeros_like(flat)
    for n in range(count):
        for r in range(ROWS):
            flat[8 * r : 8 * r + STRIP, :] = ins[n][r].astype(jnp.float32)
        for part in range(8):
            lanes = flat[:, 512 * part : 512 * part + 512].astype(jnp.bfloat16)
            made = jnp.dot(perm, lanes, preferred_element_type=jnp.float32).astype(jnp.bfloat16)
            for j in range(4):
                piece = made[:, HD * j : HD * j + HD]
                if count == 1:
                    out_ref[4 * part + j] = piece
                else:
                    out_ref[n, 4 * part + j] = piece


def pack(*arrays):
    count = len(arrays)
    lead = (count,) if count > 1 else ()
    return pl.pallas_call(
        lambda *refs: pack_body(count, *refs),
        out_shape=jax.ShapeDtypeStruct(lead + (HEADS, PIECE, HD), jnp.bfloat16),
        scratch_shapes=[pltpu.VMEM((64, HEADS * HD), jnp.float32)],
        compiler_params=pltpu.CompilerParams(vmem_limit_bytes=16 << 20),
        cost_estimate=pl.CostEstimate(flops=count * 25_000_000, bytes_accessed=count * 800_000, transcendentals=0),
        name="pack",
    )(*arrays)


def unpack_body(in_ref, out_ref):
    row = lax.broadcasted_iota(jnp.int32, (64, PIECE), 0)
    col = lax.broadcasted_iota(jnp.int32, (64, PIECE), 1)
    perm = ((col == (row % 8) * ROWS + row // 8) & (row % 8 < STRIP)).astype(jnp.bfloat16)
    for part in range(8):
        lanes = jnp.concatenate([in_ref[4 * part + j] for j in range(4)], axis=1)
        made = jnp.dot(perm, lanes, preferred_element_type=jnp.float32)
        for r in range(ROWS):
            out_ref[r, :, 512 * part : 512 * part + 512] = made[8 * r : 8 * r + STRIP].astype(jnp.bfloat16)


def unpack(array):
    return pl.pallas_call(
        unpack_body,
        out_shape=jax.ShapeDtypeStruct((ROWS, STRIP, HEADS * HD), jnp.bfloat16),
        compiler_params=pltpu.CompilerParams(vmem_limit_bytes=16 << 20),
        cost_estimate=pl.CostEstimate(flops=25_000_000, bytes_accessed=800_000, transcendentals=0),
        name="unpack",
    )(array)


def assemble(full, refs):
    for d, ref in enumerate(refs):

        def fill(i, carry, d=d, ref=ref):
            for p in range(8):
                full[d, i, PIECE * p : PIECE * p + PIECE, :] = ref[p % 2, i * 4 + p // 2]
            return carry

        lax.fori_loop(0, 8, fill, 0)


def groups(step, core):
    b, half = step // 2, step % 2
    flip = 1 - core
    return b, half, (
        (3, 0, core, 0, 2 * core),
        (2, 192, flip, 16 * core, 1),
        (1, 320, flip, 32 * flip, 2 * flip),
    )


def key_tile(win_ref, frame, frames, b, c, w):
    dt, kb, kc = win_ref[w, 0], b + win_ref[w, 1], c + win_ref[w, 2]
    kt = frame + dt
    live = (kt >= 0) & (kt < frames) & (kb >= 0) & (kb < 2) & (kc >= 0) & (kc < COLS)
    return live, dt + 1, kb, kc


def tile_rows(full, d, kb, kc):
    start = pl.multiple_of(kc * CHUNK, CHUNK)
    return jnp.concatenate([full[d, 2 * f + kb, pl.ds(start, CHUNK), :] for f in range(4)], axis=0)


def score_body(frames, win_ref, pos_ref, q_ref, back_ref, own_ref, next_ref, p_ref, l_ref, keys, s_ref, m_ref):
    step = pl.program_id(0)
    frame, core = pos_ref[0], pos_ref[1]

    @pl.when(step == 0)
    def _():
        assemble(keys, (back_ref, own_ref, next_ref))

    b, half, parts = groups(step, core)
    for size, base, j, first, t in parts:
        count = CHUNK * size
        c = 3 * half + t
        first = pl.multiple_of(first, 16)
        q = jnp.concatenate(
            [q_ref[(2 * f + b) * 4 + 2 * half + j, pl.ds(first, 16 * size), :] for f in range(4)], axis=0
        )
        m_ref[0:count, :] = jnp.full((count, HD), LOW, jnp.float32)

        def score(w, carry, q=q, count=count, c=c):
            live, d, kb, kc = key_tile(win_ref, frame, frames, b, c, w)

            @pl.when(live)
            def _():
                k = tile_rows(keys, d, kb, kc)
                s = lax.dot_general(q, k, (((1,), (1,)), ((), ())), preferred_element_type=jnp.float32)
                s_ref[w, 0:count, :] = s
                m_ref[0:count, :] = jnp.maximum(m_ref[0:count, :], jnp.maximum(s[:, :HD], s[:, HD:]))

            return carry

        lax.fori_loop(0, WIN, score, 0)
        top = jnp.max(m_ref[0:count, :], axis=1, keepdims=True)
        l_ref[0, base : base + count, :] = jnp.zeros((count, HD), jnp.float32)

        def weigh(w, carry, top=top, count=count, c=c, base=base):
            live, _, _, _ = key_tile(win_ref, frame, frames, b, c, w)

            @pl.when(live)
            def _():
                p = jnp.exp2((s_ref[w, 0:count, :] - top) * C2)
                l_ref[0, base : base + count, :] += p[:, :HD] + p[:, HD:]
                p_ref[0, w, base : base + count, :] = p.astype(jnp.bfloat16)

            return carry

        lax.fori_loop(0, WIN, weigh, 0)
        total = jnp.sum(l_ref[0, base : base + count, :], axis=1, keepdims=True)
        l_ref[0, base : base + count, :] = jnp.broadcast_to(1.0 / total, (count, HD))


def mix_body(frames, win_ref, pos_ref, p_ref, l_ref, back_ref, own_ref, next_ref, out_ref, values, o_ref):
    step = pl.program_id(0)
    frame, core = pos_ref[0], pos_ref[1]

    @pl.when(step == 0)
    def _():
        assemble(values, (back_ref, own_ref, next_ref))

    b, half, parts = groups(step, core)
    for size, base, j, first, t in parts:
        count = CHUNK * size
        c = 3 * half + t
        first = pl.multiple_of(first, 16)
        o_ref[0:count, :] = jnp.zeros((count, HD), jnp.float32)

        def mix(w, carry, count=count, c=c, base=base):
            live, d, kb, kc = key_tile(win_ref, frame, frames, b, c, w)

            @pl.when(live)
            def _():
                v = tile_rows(values, d, kb, kc)
                o_ref[0:count, :] += jnp.dot(
                    p_ref[0, w, base : base + count, :], v, preferred_element_type=jnp.float32
                )

            return carry

        lax.fori_loop(0, WIN, mix, 0)
        o = (o_ref[0:count, :] * l_ref[0, base : base + count, :]).astype(jnp.bfloat16)
        for f in range(4):
            out_ref[(2 * f + b) * 4 + 2 * half + j, pl.ds(first, 16 * size), :] = o[16 * size * f : 16 * size * (f + 1)]


def whole(*shape):
    return pl.BlockSpec(shape, lambda g, *_: (0,) * len(shape))


def scores(window, pos, q, back, own, following, frames):
    return pl.pallas_call(
        lambda *refs: score_body(frames, *refs),
        out_shape=(
            jax.ShapeDtypeStruct((4, WIN, 384, TILE), jnp.bfloat16),
            jax.ShapeDtypeStruct((4, 384, HD), jnp.float32),
        ),
        grid_spec=pltpu.PrefetchScalarGridSpec(
            num_scalar_prefetch=2,
            grid=(4,),
            in_specs=[whole(CHIPS, PIECE, HD)] + [whole(2, CHIPS, PIECE, HD)] * 3,
            out_specs=(
                pl.BlockSpec((1, WIN, 384, TILE), lambda g, *_: (g, 0, 0, 0)),
                pl.BlockSpec((1, 384, HD), lambda g, *_: (g, 0, 0)),
            ),
            scratch_shapes=[
                pltpu.VMEM((3, 8, SPAN, HD), jnp.bfloat16),
                pltpu.VMEM((WIN, 192, TILE), jnp.float32),
                pltpu.VMEM((192, HD), jnp.float32),
            ],
        ),
        compiler_params=pltpu.CompilerParams(vmem_limit_bytes=28 << 20),
        cost_estimate=pl.CostEstimate(flops=810_000_000, bytes_accessed=10_000_000, transcendentals=3_200_000),
        name="scores",
    )(window, pos, q, back, own, following)


def mix(window, pos, p, l, back, own, following, frames):
    return pl.pallas_call(
        lambda *refs: mix_body(frames, *refs),
        out_shape=jax.ShapeDtypeStruct((CHIPS, PIECE, HD), jnp.bfloat16),
        grid_spec=pltpu.PrefetchScalarGridSpec(
            num_scalar_prefetch=2,
            grid=(4,),
            in_specs=[
                pl.BlockSpec((1, WIN, 384, TILE), lambda g, *_: (g, 0, 0, 0)),
                pl.BlockSpec((1, 384, HD), lambda g, *_: (g, 0, 0)),
            ]
            + [whole(2, CHIPS, PIECE, HD)] * 3,
            out_specs=whole(CHIPS, PIECE, HD),
            scratch_shapes=[
                pltpu.VMEM((3, 8, SPAN, HD), jnp.bfloat16),
                pltpu.VMEM((192, HD), jnp.float32),
            ],
        ),
        compiler_params=pltpu.CompilerParams(vmem_limit_bytes=28 << 20),
        cost_estimate=pl.CostEstimate(flops=810_000_000, bytes_accessed=10_000_000, transcendentals=0),
        name="mix",
    )(window, pos, p, l, back, own, following)


def per_device(query_rows, key_rows, value_rows, window_offsets):
    frames = lax.axis_size("a")
    later = [(j, j + 1) for j in range(frames - 1)]
    earlier = [(j + 1, j) for j in range(frames - 1)]
    pos = jnp.stack([lax.axis_index("a"), lax.axis_index("core")]).astype(jnp.int32)
    k = lax.all_to_all(pack(key_rows), ("i", "y"), 0, 0, tiled=True)
    k_back = lax.ppermute(k, "a", later)
    k_next = lax.ppermute(k, "a", earlier)
    vq = lax.all_to_all(pack(value_rows, query_rows), ("i", "y"), 1, 1, tiled=True)
    v, q = vq[0], vq[1]
    v_back = lax.ppermute(v, "a", later)
    v_next = lax.ppermute(v, "a", earlier)
    k_all = [lax.all_gather(x, "core") for x in (k_back, k, k_next)]
    v_all = [lax.all_gather(x, "core") for x in (v_back, v, v_next)]
    p, l = scores(window_offsets, pos, q, *k_all, frames)
    out = mix(window_offsets, pos, p, l, *v_all, frames)
    return unpack(lax.all_to_all(out, ("i", "y"), 0, 0, tiled=True))


def solution(mesh):
    slabs, strips = mesh.devices.shape
    fine = Mesh(mesh.devices.reshape(slabs // 8, 8, strips // 2, 2), ("a", "i", "y", "core"))
    spec = P(("a", "i"), ("y", "core"), None)
    return jax.shard_map(
        per_device,
        mesh=fine,
        in_specs=(spec, spec, spec, P()),
        out_specs=spec,
        check_vma=False,
    )
```

```python
import jax
import jax.numpy as jnp
from jax import lax
from jax.experimental import pallas as pl
from jax.experimental.pallas import tpu as pltpu
from jax.sharding import Mesh, PartitionSpec as P

HD = 128
HEADS = 32
STRIP = 6
ROWS = 8
PIECE = STRIP * ROWS
SPAN = 8 * PIECE
CHUNK = 64
TILE = 256
COLS = 6
WIN = 8
CHIPS = 32
C2 = HD ** (-0.5) * 1.4426950408889634


def pack_body(*refs):
    ins, out_ref = refs[:-1], refs[-1]
    for n, ref in enumerate(ins):
        for h in range(HEADS // 4):
            piece = ref[:, :, HD * h : HD * h + HD].astype(jnp.float32)
            out_ref[h, n] = piece.reshape(PIECE, HD).astype(jnp.bfloat16)


def pack(*arrays):
    count = len(arrays)
    arrays = [pltpu.with_memory_space_constraint(x, pltpu.HBM) for x in arrays]
    return pl.pallas_call(
        pack_body,
        out_shape=jax.ShapeDtypeStruct((HEADS, count, PIECE, HD), jnp.bfloat16),
        grid=(4,),
        in_specs=[pl.BlockSpec((STRIP, ROWS, HEADS * HD // 4), lambda g: (0, 0, g))] * count,
        out_specs=pl.BlockSpec((HEADS // 4, count, PIECE, HD), lambda g: (g, 0, 0, 0)),
        compiler_params=pltpu.CompilerParams(vmem_limit_bytes=16 << 20),
        cost_estimate=pl.CostEstimate(flops=0, bytes_accessed=count * 800_000, transcendentals=0),
        name="pack",
    )(*arrays)


def unpack_body(in_ref, out_ref):
    for h in range(HEADS):
        piece = in_ref[h].astype(jnp.float32).reshape(STRIP, ROWS, HD)
        out_ref[:, :, HD * h : HD * h + HD] = piece.astype(jnp.bfloat16)


def unpack(array):
    return pl.pallas_call(
        unpack_body,
        out_shape=jax.ShapeDtypeStruct((STRIP, ROWS, HEADS * HD), jnp.bfloat16),
        compiler_params=pltpu.CompilerParams(vmem_limit_bytes=16 << 20),
        cost_estimate=pl.CostEstimate(flops=0, bytes_accessed=800_000, transcendentals=0),
        name="unpack",
    )(array)


def assemble(full, own_ref, near_ref, far_ref):
    def fill(i, carry):
        for ref, frame, swap in ((own_ref, 1, 0), (near_ref, None, 0), (far_ref, None, 1)):
            for c in range(2):
                for y in range(4):
                    p = 2 * y + (c ^ swap)
                    d = 2 * c if frame is None else frame
                    full[d, i, PIECE * p : PIECE * p + PIECE, :] = ref[c, i * 4 + y]
        return carry

    lax.fori_loop(0, 8, fill, 0)


def groups(step, core):
    b, half = step // 2, step % 2
    flip = 1 - core
    return b, half, (
        (3, 0, core, 0, 2 * core),
        (2, 192, flip, 16 * core, 1),
        (1, 320, flip, 32 * flip, 2 * flip),
    )


def key_tile(win_ref, frame, frames, b, c, w):
    dt, kb, kc = win_ref[w, 0], b + win_ref[w, 1], c + win_ref[w, 2]
    kt = frame + dt
    live = (kt >= 0) & (kt < frames) & (kb >= 0) & (kb < 2) & (kc >= 0) & (kc < COLS)
    return live, dt + 1, kb, kc


def tile_rows(full, d, kb, kc):
    start = pl.multiple_of(kc * CHUNK, CHUNK)
    return jnp.concatenate([full[d, 2 * f + kb, pl.ds(start, CHUNK), :] for f in range(4)], axis=0)


def score_body(frames, win_ref, pos_ref, q_ref, own_ref, near_ref, far_ref, p_ref, l_ref, keys, s_ref):
    frame, core = pos_ref[0], pos_ref[1]
    assemble(keys, own_ref, near_ref, far_ref)

    def step_body(step, carry):
        b, half, parts = groups(step, core)
        for size, base, j, first, t in parts:
            count = CHUNK * size
            c = 3 * half + t
            first = pl.multiple_of(first, 16)
            q = jnp.concatenate(
                [q_ref[(2 * f + b) * 4 + 2 * half + j, pl.ds(first, 16 * size), :] for f in range(4)], axis=0
            )
            most = None
            lives = []
            for w in range(WIN):
                live, d, kb, kc = key_tile(win_ref, frame, frames, b, c, w)
                lives.append(live)
                k = tile_rows(keys, jnp.where(live, d, 1), jnp.where(live, kb, b), jnp.where(live, kc, c))
                s = lax.dot_general(q, k, (((1,), (1,)), ((), ())), preferred_element_type=jnp.float32)
                s_ref[w, 0:count, :] = s
                high = jnp.maximum(s[:, :HD], s[:, HD:])
                most = high if most is None else jnp.maximum(most, high)
            top = jnp.max(most, axis=1, keepdims=True)
            total = jnp.zeros((count, HD), jnp.float32)
            for w in range(WIN):
                p = jnp.exp2((s_ref[w, 0:count, :] - top) * C2)
                total += jnp.where(lives[w], p[:, :HD] + p[:, HD:], 0.0)
                p_ref[step, w, base : base + count, :] = p.astype(jnp.bfloat16)
            total = jnp.sum(total, axis=1, keepdims=True)
            l_ref[step, base : base + count, :] = jnp.broadcast_to(1.0 / total, (count, HD))
        return carry

    lax.fori_loop(0, 4, step_body, 0)


def mix_body(frames, win_ref, pos_ref, p_ref, l_ref, own_ref, near_ref, far_ref, out_ref, values):
    frame, core = pos_ref[0], pos_ref[1]
    assemble(values, own_ref, near_ref, far_ref)
    for f in range(4):
        values[3, 2 * f, 0:CHUNK, :] = jnp.zeros((CHUNK, HD), jnp.bfloat16)

    def step_body(step, carry):
        b, half, parts = groups(step, core)
        for size, base, j, first, t in parts:
            count = CHUNK * size
            c = 3 * half + t
            first = pl.multiple_of(first, 16)
            o = jnp.zeros((count, HD), jnp.float32)
            for w in range(WIN):
                live, d, kb, kc = key_tile(win_ref, frame, frames, b, c, w)
                v = tile_rows(values, jnp.where(live, d, 3), jnp.where(live, kb, 0), jnp.where(live, kc, 0))
                o += jnp.dot(p_ref[step, w, base : base + count, :], v, preferred_element_type=jnp.float32)
            o = (o * l_ref[step, base : base + count, :]).astype(jnp.bfloat16)
            for f in range(4):
                out_ref[(2 * f + b) * 4 + 2 * half + j, pl.ds(first, 16 * size), :] = o[
                    16 * size * f : 16 * size * (f + 1)
                ]
        return carry

    lax.fori_loop(0, 4, step_body, 0)


SMALL = pl.BlockSpec(memory_space=pltpu.SMEM)
LOCAL = pl.BlockSpec(memory_space=pltpu.VMEM)


def scores(window, pos, q, own, near, far, frames):
    return pl.pallas_call(
        lambda *refs: score_body(frames, *refs),
        out_shape=(
            jax.ShapeDtypeStruct((4, WIN, 384, TILE), jnp.bfloat16),
            jax.ShapeDtypeStruct((4, 384, HD), jnp.float32),
        ),
        in_specs=[SMALL] * 2 + [LOCAL] * 4,
        out_specs=(LOCAL, LOCAL),
        scratch_shapes=[
            pltpu.VMEM((3, 8, SPAN, HD), jnp.bfloat16),
            pltpu.VMEM((WIN, 192, TILE), jnp.float32),
        ],
        compiler_params=pltpu.CompilerParams(vmem_limit_bytes=24 << 20),
        cost_estimate=pl.CostEstimate(flops=1_000_000, bytes_accessed=1_000_000, transcendentals=0),
        name="scores",
    )(window, pos, q, own, near, far)


def mix(window, pos, p, l, own, near, far, frames):
    return pl.pallas_call(
        lambda *refs: mix_body(frames, *refs),
        out_shape=jax.ShapeDtypeStruct((CHIPS, PIECE, HD), jnp.bfloat16),
        in_specs=[SMALL] * 2 + [LOCAL] * 5,
        out_specs=LOCAL,
        scratch_shapes=[pltpu.VMEM((4, 8, SPAN, HD), jnp.bfloat16)],
        compiler_params=pltpu.CompilerParams(vmem_limit_bytes=24 << 20),
        cost_estimate=pl.CostEstimate(flops=810_000_000, bytes_accessed=10_000_000, transcendentals=0),
        name="mix",
    )(window, pos, p, l, own, near, far)


def rim(strips, frames):
    pairs = [(2 * j, 2 * j + 2) for j in range(frames - 1)] + [(2 * j + 3, 2 * j + 1) for j in range(frames - 1)]
    return lax.ppermute(strips, ("a", "core"), pairs)


def both(strips):
    return lax.all_gather(strips, "core")


def per_device(query_rows, key_rows, value_rows, window_offsets):
    frames, core = lax.axis_size("a"), lax.axis_index("core")
    pos = jnp.stack([lax.axis_index("a"), core]).astype(jnp.int32)
    by_column = [x.transpose(1, 0, 2) for x in (key_rows, value_rows, query_rows)]
    kvq = lax.all_to_all(pack(*by_column), ("i", "y"), 0, 0, tiled=True)
    k, v, q = kvq[:, 0], kvq[:, 1], kvq[:, 2]
    k_near = rim(k, frames)
    k_both = both(k)
    k_far = rim(lax.dynamic_index_in_dim(k_both, 1 - core, keepdims=False), frames)
    v_both = both(v)
    v_other = lax.dynamic_index_in_dim(v_both, 1 - core, keepdims=False)
    k_near, v = lax.optimization_barrier((k_near, v))
    v_near = rim(v, frames)
    k_far, v_other = lax.optimization_barrier((k_far, v_other))
    v_far = rim(v_other, frames)
    p, l = scores(window_offsets, pos, q, k_both, both(k_near), both(k_far), frames)
    p, v_near, v_far = lax.optimization_barrier((p, v_near, v_far))
    out = mix(window_offsets, pos, p, l, v_both, both(v_near), both(v_far), frames)
    return unpack(lax.all_to_all(out, ("i", "y"), 0, 0, tiled=True)).transpose(1, 0, 2)


def solution(mesh):
    slabs, strips = mesh.devices.shape
    fine = Mesh(mesh.devices.reshape(slabs // 8, 8, strips // 2, 2), ("a", "i", "y", "core"))
    spec = P(("a", "i"), ("y", "core"), None)
    return jax.shard_map(
        per_device,
        mesh=fine,
        in_specs=(spec, spec, spec, P()),
        out_specs=spec,
        check_vma=False,
    )
```

```python
import jax
import jax.numpy as jnp
from jax import lax
from jax.experimental import pallas as pl
from jax.experimental.pallas import tpu as pltpu
from jax.sharding import Mesh, PartitionSpec as P

HD = 128
HEADS = 32
STRIP = 6
ROWS = 8
PIECE = STRIP * ROWS
SPAN = 8 * PIECE
CHUNK = 64
TILE = 256
COLS = 6
WIN = 8
CHIPS = 32
C2 = HD ** (-0.5) * 1.4426950408889634


def pack_body(*refs):
    count = len(refs) // 2 - 1
    ins, out_ref, held, sems = refs[:count], refs[count], refs[count + 1 : -1], refs[-1]
    copies = [pltpu.make_async_copy(ins[n], held[n], sems.at[n]) for n in range(count)]
    for copy in copies:
        copy.start()
    for n in range(count):
        copies[n].wait()
        for h in range(HEADS):
            piece = held[n][:, :, HD * h : HD * h + HD].astype(jnp.float32)
            out_ref[h, n] = piece.reshape(PIECE, HD).astype(jnp.bfloat16)


def pack(*arrays):
    count = len(arrays)
    arrays = [pltpu.with_memory_space_constraint(x, pltpu.HBM) for x in arrays]
    return pl.pallas_call(
        pack_body,
        out_shape=jax.ShapeDtypeStruct((HEADS, count, PIECE, HD), jnp.bfloat16),
        in_specs=[pl.BlockSpec(memory_space=pltpu.HBM)] * count,
        out_specs=pl.BlockSpec(memory_space=pltpu.VMEM),
        scratch_shapes=[pltpu.VMEM((STRIP, ROWS, HEADS * HD), jnp.bfloat16)] * count
        + [pltpu.SemaphoreType.DMA((count,))],
        compiler_params=pltpu.CompilerParams(vmem_limit_bytes=16 << 20),
        cost_estimate=pl.CostEstimate(flops=0, bytes_accessed=count * 800_000, transcendentals=0),
        name="pack",
    )(*arrays)


def unpack_body(in_ref, out_ref):
    for h in range(HEADS):
        piece = in_ref[h].astype(jnp.float32).reshape(STRIP, ROWS, HD)
        out_ref[:, :, HD * h : HD * h + HD] = piece.astype(jnp.bfloat16)


def unpack(array):
    return pl.pallas_call(
        unpack_body,
        out_shape=jax.ShapeDtypeStruct((STRIP, ROWS, HEADS * HD), jnp.bfloat16),
        compiler_params=pltpu.CompilerParams(vmem_limit_bytes=16 << 20),
        cost_estimate=pl.CostEstimate(flops=0, bytes_accessed=800_000, transcendentals=0),
        name="unpack",
    )(array)


def assemble(full, own_ref, near_ref, far_ref):
    def fill(i, carry):
        for ref, frame, swap in ((own_ref, 1, 0), (near_ref, None, 0), (far_ref, None, 1)):
            for c in range(2):
                for y in range(4):
                    p = 2 * y + (c ^ swap)
                    d = 2 * c if frame is None else frame
                    full[d, i, PIECE * p : PIECE * p + PIECE, :] = ref[c, i * 4 + y]
        return carry

    lax.fori_loop(0, 8, fill, 0)


def groups(step, core):
    b, half = step // 2, step % 2
    flip = 1 - core
    return b, half, (
        (3, 0, core, 0, 2 * core),
        (2, 192, flip, 16 * core, 1),
        (1, 320, flip, 32 * flip, 2 * flip),
    )


def key_tile(win_ref, frame, frames, b, c, w):
    dt, kb, kc = win_ref[w, 0], b + win_ref[w, 1], c + win_ref[w, 2]
    kt = frame + dt
    live = (kt >= 0) & (kt < frames) & (kb >= 0) & (kb < 2) & (kc >= 0) & (kc < COLS)
    return live, dt + 1, kb, kc


def tile_rows(full, d, kb, kc):
    start = pl.multiple_of(kc * CHUNK, CHUNK)
    return jnp.concatenate([full[d, 2 * f + kb, pl.ds(start, CHUNK), :] for f in range(4)], axis=0)


def score_body(frames, win_ref, pos_ref, q_ref, own_ref, near_ref, far_ref, p_ref, l_ref, keys, s_ref):
    frame, core = pos_ref[0], pos_ref[1]
    assemble(keys, own_ref, near_ref, far_ref)

    def step_body(step, carry):
        b, half, parts = groups(step, core)
        for size, base, j, first, t in parts:
            count = CHUNK * size
            c = 3 * half + t
            first = pl.multiple_of(first, 16)
            q = jnp.concatenate(
                [q_ref[(2 * f + b) * 4 + 2 * half + j, pl.ds(first, 16 * size), :] for f in range(4)], axis=0
            )
            most = None
            lives = []
            for w in range(WIN):
                live, d, kb, kc = key_tile(win_ref, frame, frames, b, c, w)
                lives.append(live)
                k = tile_rows(keys, jnp.where(live, d, 1), jnp.where(live, kb, b), jnp.where(live, kc, c))
                s = lax.dot_general(q, k, (((1,), (1,)), ((), ())), preferred_element_type=jnp.float32)
                s_ref[w, 0:count, :] = s
                high = jnp.maximum(s[:, :HD], s[:, HD:])
                most = high if most is None else jnp.maximum(most, high)
            top = jnp.max(most, axis=1, keepdims=True)
            total = jnp.zeros((count, HD), jnp.float32)
            for w in range(WIN):
                p = jnp.exp2((s_ref[w, 0:count, :] - top) * C2)
                total += jnp.where(lives[w], p[:, :HD] + p[:, HD:], 0.0)
                p_ref[step, w, base : base + count, :] = p.astype(jnp.bfloat16)
            total = jnp.sum(total, axis=1, keepdims=True)
            l_ref[step, base : base + count, :] = jnp.broadcast_to(1.0 / total, (count, HD))
        return carry

    lax.fori_loop(0, 4, step_body, 0)


def mix_body(frames, win_ref, pos_ref, p_ref, l_ref, own_ref, near_ref, far_ref, out_ref, values):
    frame, core = pos_ref[0], pos_ref[1]
    assemble(values, own_ref, near_ref, far_ref)
    for f in range(4):
        values[3, 2 * f, 0:CHUNK, :] = jnp.zeros((CHUNK, HD), jnp.bfloat16)

    def step_body(step, carry):
        b, half, parts = groups(step, core)
        for size, base, j, first, t in parts:
            count = CHUNK * size
            c = 3 * half + t
            first = pl.multiple_of(first, 16)
            o = jnp.zeros((count, HD), jnp.float32)
            for w in range(WIN):
                live, d, kb, kc = key_tile(win_ref, frame, frames, b, c, w)
                v = tile_rows(values, jnp.where(live, d, 3), jnp.where(live, kb, 0), jnp.where(live, kc, 0))
                o += jnp.dot(p_ref[step, w, base : base + count, :], v, preferred_element_type=jnp.float32)
            o = (o * l_ref[step, base : base + count, :]).astype(jnp.bfloat16)
            for f in range(4):
                out_ref[(2 * f + b) * 4 + 2 * half + j, pl.ds(first, 16 * size), :] = o[
                    16 * size * f : 16 * size * (f + 1)
                ]
        return carry

    lax.fori_loop(0, 4, step_body, 0)


SMALL = pl.BlockSpec(memory_space=pltpu.SMEM)
LOCAL = pl.BlockSpec(memory_space=pltpu.VMEM)


def scores(window, pos, q, own, near, far, frames):
    return pl.pallas_call(
        lambda *refs: score_body(frames, *refs),
        out_shape=(
            jax.ShapeDtypeStruct((4, WIN, 384, TILE), jnp.bfloat16),
            jax.ShapeDtypeStruct((4, 384, HD), jnp.float32),
        ),
        in_specs=[SMALL] * 2 + [LOCAL] * 4,
        out_specs=(LOCAL, LOCAL),
        scratch_shapes=[
            pltpu.VMEM((3, 8, SPAN, HD), jnp.bfloat16),
            pltpu.VMEM((WIN, 192, TILE), jnp.float32),
        ],
        compiler_params=pltpu.CompilerParams(vmem_limit_bytes=24 << 20),
        cost_estimate=pl.CostEstimate(flops=1_000_000, bytes_accessed=1_000_000, transcendentals=0),
        name="scores",
    )(window, pos, q, own, near, far)


def mix(window, pos, p, l, own, near, far, frames):
    return pl.pallas_call(
        lambda *refs: mix_body(frames, *refs),
        out_shape=jax.ShapeDtypeStruct((CHIPS, PIECE, HD), jnp.bfloat16),
        in_specs=[SMALL] * 2 + [LOCAL] * 5,
        out_specs=LOCAL,
        scratch_shapes=[pltpu.VMEM((4, 8, SPAN, HD), jnp.bfloat16)],
        compiler_params=pltpu.CompilerParams(vmem_limit_bytes=24 << 20),
        cost_estimate=pl.CostEstimate(flops=810_000_000, bytes_accessed=10_000_000, transcendentals=0),
        name="mix",
    )(window, pos, p, l, own, near, far)


def rim(strips, frames):
    pairs = [(2 * j, 2 * j + 2) for j in range(frames - 1)] + [(2 * j + 3, 2 * j + 1) for j in range(frames - 1)]
    return lax.ppermute(strips, ("a", "core"), pairs)


def both(strips):
    return lax.all_gather(strips, "core")


def per_device(query_rows, key_rows, value_rows, window_offsets):
    frames, core = lax.axis_size("a"), lax.axis_index("core")
    pos = jnp.stack([lax.axis_index("a"), core]).astype(jnp.int32)
    by_column = [x.transpose(1, 0, 2) for x in (key_rows, value_rows, query_rows)]
    kvq = lax.all_to_all(pack(*by_column), ("i", "y"), 0, 0, tiled=True)
    k, v, q = kvq[:, 0], kvq[:, 1], kvq[:, 2]
    k_near = rim(k, frames)
    k_both = both(k)
    k_far = rim(lax.dynamic_index_in_dim(k_both, 1 - core, keepdims=False), frames)
    v_both = both(v)
    v_other = lax.dynamic_index_in_dim(v_both, 1 - core, keepdims=False)
    k_near, v = lax.optimization_barrier((k_near, v))
    v_near, k_near = rim(v, frames), both(k_near)
    k_near, k_far, v_other = lax.optimization_barrier((k_near, k_far, v_other))
    v_far, k_far = rim(v_other, frames), both(k_far)
    p, l = scores(window_offsets, pos, q, k_both, k_near, k_far, frames)
    p, v_near = lax.optimization_barrier((p, v_near))
    v_near = both(v_near)
    v_near, v_far = lax.optimization_barrier((v_near, v_far))
    out = mix(window_offsets, pos, p, l, v_both, v_near, both(v_far), frames)
    return unpack(lax.all_to_all(out, ("i", "y"), 0, 0, tiled=True)).transpose(1, 0, 2)


def solution(mesh):
    slabs, strips = mesh.devices.shape
    fine = Mesh(mesh.devices.reshape(slabs // 8, 8, strips // 2, 2), ("a", "i", "y", "core"))
    spec = P(("a", "i"), ("y", "core"), None)
    return jax.shard_map(
        per_device,
        mesh=fine,
        in_specs=(spec, spec, spec, P()),
        out_specs=spec,
        check_vma=False,
    )
```

```python
import jax
import jax.numpy as jnp
from jax import lax
from jax.experimental import pallas as pl
from jax.experimental.pallas import tpu as pltpu
from jax.sharding import Mesh, PartitionSpec as P

HD = 128
HEADS = 32
STRIP = 6
ROWS = 8
PIECE = STRIP * ROWS
SPAN = 8 * PIECE
CHUNK = 64
TILE = 256
COLS = 6
WIN = 8
CHIPS = 32
C2 = HD ** (-0.5) * 1.4426950408889634


def pack_body(*refs):
    count = len(refs) // 2 - 1
    ins, out_ref, held, sems = refs[:count], refs[count], refs[count + 1 : -1], refs[-1]
    copies = [pltpu.make_async_copy(ins[n], held[n], sems.at[n]) for n in range(count)]
    for copy in copies:
        copy.start()
    for n in range(count):
        copies[n].wait()
        for h in range(HEADS):
            piece = held[n][:, :, HD * h : HD * h + HD].astype(jnp.float32)
            out_ref[h, n] = piece.reshape(PIECE, HD).astype(jnp.bfloat16)


def pack(*arrays):
    count = len(arrays)
    arrays = [pltpu.with_memory_space_constraint(x, pltpu.HBM) for x in arrays]
    return pl.pallas_call(
        pack_body,
        out_shape=jax.ShapeDtypeStruct((HEADS, count, PIECE, HD), jnp.bfloat16),
        in_specs=[pl.BlockSpec(memory_space=pltpu.HBM)] * count,
        out_specs=pl.BlockSpec(memory_space=pltpu.VMEM),
        scratch_shapes=[pltpu.VMEM((STRIP, ROWS, HEADS * HD), jnp.bfloat16)] * count
        + [pltpu.SemaphoreType.DMA((count,))],
        compiler_params=pltpu.CompilerParams(vmem_limit_bytes=16 << 20),
        cost_estimate=pl.CostEstimate(flops=0, bytes_accessed=count * 800_000, transcendentals=0),
        name="pack",
    )(*arrays)


def unpack_body(in_ref, out_ref):
    for h in range(HEADS):
        piece = in_ref[h].astype(jnp.float32).reshape(STRIP, ROWS, HD)
        out_ref[:, :, HD * h : HD * h + HD] = piece.astype(jnp.bfloat16)


def unpack(array):
    return pl.pallas_call(
        unpack_body,
        out_shape=jax.ShapeDtypeStruct((STRIP, ROWS, HEADS * HD), jnp.bfloat16),
        compiler_params=pltpu.CompilerParams(vmem_limit_bytes=16 << 20),
        cost_estimate=pl.CostEstimate(flops=0, bytes_accessed=800_000, transcendentals=0),
        name="unpack",
    )(array)


def assemble(full, own_ref, near_ref, far_ref):
    def fill(i, carry):
        for ref, frame, swap in ((own_ref, 1, 0), (near_ref, None, 0), (far_ref, None, 1)):
            for c in range(2):
                for y in range(4):
                    p = 2 * y + (c ^ swap)
                    d = 2 * c if frame is None else frame
                    full[d, i, PIECE * p : PIECE * p + PIECE, :] = ref[c, i * 4 + y]
        return carry

    lax.fori_loop(0, 8, fill, 0)


def groups(step, core):
    b, half = step // 2, step % 2
    flip = 1 - core
    return b, half, (
        (3, 0, core, 0, 2 * core),
        (2, 192, flip, 16 * core, 1),
        (1, 320, flip, 32 * flip, 2 * flip),
    )


def key_tile(win_ref, frame, frames, b, c, w):
    dt, kb, kc = win_ref[w, 0], b + win_ref[w, 1], c + win_ref[w, 2]
    kt = frame + dt
    live = (kt >= 0) & (kt < frames) & (kb >= 0) & (kb < 2) & (kc >= 0) & (kc < COLS)
    return live, dt + 1, kb, kc


def tile_rows(full, d, kb, kc):
    start = pl.multiple_of(kc * CHUNK, CHUNK)
    return jnp.concatenate([full[d, 2 * f + kb, pl.ds(start, CHUNK), :] for f in range(4)], axis=0)


def score_body(frames, win_ref, pos_ref, q_ref, own_ref, near_ref, far_ref, p_ref, l_ref, keys, s_ref):
    frame, core = pos_ref[0], pos_ref[1]
    assemble(keys, own_ref, near_ref, far_ref)

    def step_body(step, carry):
        b, half, parts = groups(step, core)
        for size, base, j, first, t in parts:
            count = CHUNK * size
            c = 3 * half + t
            first = pl.multiple_of(first, 16)
            q = jnp.concatenate(
                [q_ref[(2 * f + b) * 4 + 2 * half + j, pl.ds(first, 16 * size), :] for f in range(4)], axis=0
            )
            most = None
            lives = []
            for w in range(WIN):
                live, d, kb, kc = key_tile(win_ref, frame, frames, b, c, w)
                lives.append(live)
                k = tile_rows(keys, jnp.where(live, d, 1), jnp.where(live, kb, b), jnp.where(live, kc, c))
                s = lax.dot_general(q, k, (((1,), (1,)), ((), ())), preferred_element_type=jnp.float32)
                s_ref[w, 0:count, :] = s
                high = jnp.maximum(s[:, :HD], s[:, HD:])
                most = high if most is None else jnp.maximum(most, high)
            top = jnp.max(most, axis=1, keepdims=True)
            total = jnp.zeros((count, HD), jnp.float32)
            for w in range(WIN):
                p = jnp.exp2((s_ref[w, 0:count, :] - top) * C2)
                total += jnp.where(lives[w], p[:, :HD] + p[:, HD:], 0.0)
                p_ref[step, base : base + count, TILE * w : TILE * w + TILE] = p.astype(jnp.bfloat16)
            total = jnp.sum(total, axis=1, keepdims=True)
            l_ref[step, base : base + count, :] = jnp.broadcast_to(1.0 / total, (count, HD))
        return carry

    lax.fori_loop(0, 4, step_body, 0)


def mix_body(frames, win_ref, pos_ref, p_ref, l_ref, own_ref, near_ref, far_ref, out_ref, values):
    frame, core = pos_ref[0], pos_ref[1]
    assemble(values, own_ref, near_ref, far_ref)
    for f in range(4):
        values[3, 2 * f, 0:CHUNK, :] = jnp.zeros((CHUNK, HD), jnp.bfloat16)

    def step_body(step, carry):
        b, half, parts = groups(step, core)
        for size, base, j, first, t in parts:
            count = CHUNK * size
            c = 3 * half + t
            first = pl.multiple_of(first, 16)
            tiles = []
            for w in range(WIN):
                live, d, kb, kc = key_tile(win_ref, frame, frames, b, c, w)
                tiles.append(tile_rows(values, jnp.where(live, d, 3), jnp.where(live, kb, 0), jnp.where(live, kc, 0)))
            o = jnp.dot(
                p_ref[step, base : base + count, :], jnp.concatenate(tiles, axis=0), preferred_element_type=jnp.float32
            )
            o = (o * l_ref[step, base : base + count, :]).astype(jnp.bfloat16)
            for f in range(4):
                out_ref[(2 * f + b) * 4 + 2 * half + j, pl.ds(first, 16 * size), :] = o[
                    16 * size * f : 16 * size * (f + 1)
                ]
        return carry

    lax.fori_loop(0, 4, step_body, 0)


SMALL = pl.BlockSpec(memory_space=pltpu.SMEM)
LOCAL = pl.BlockSpec(memory_space=pltpu.VMEM)


def scores(window, pos, q, own, near, far, frames):
    return pl.pallas_call(
        lambda *refs: score_body(frames, *refs),
        out_shape=(
            jax.ShapeDtypeStruct((4, 384, WIN * TILE), jnp.bfloat16),
            jax.ShapeDtypeStruct((4, 384, HD), jnp.float32),
        ),
        in_specs=[SMALL] * 2 + [LOCAL] * 4,
        out_specs=(LOCAL, LOCAL),
        scratch_shapes=[
            pltpu.VMEM((3, 8, SPAN, HD), jnp.bfloat16),
            pltpu.VMEM((WIN, 192, TILE), jnp.float32),
        ],
        compiler_params=pltpu.CompilerParams(vmem_limit_bytes=24 << 20),
        cost_estimate=pl.CostEstimate(flops=1_000_000, bytes_accessed=1_000_000, transcendentals=0),
        name="scores",
    )(window, pos, q, own, near, far)


def mix(window, pos, p, l, own, near, far, frames):
    return pl.pallas_call(
        lambda *refs: mix_body(frames, *refs),
        out_shape=jax.ShapeDtypeStruct((CHIPS, PIECE, HD), jnp.bfloat16),
        in_specs=[SMALL] * 2 + [LOCAL] * 5,
        out_specs=LOCAL,
        scratch_shapes=[pltpu.VMEM((4, 8, SPAN, HD), jnp.bfloat16)],
        compiler_params=pltpu.CompilerParams(vmem_limit_bytes=24 << 20),
        cost_estimate=pl.CostEstimate(flops=810_000_000, bytes_accessed=10_000_000, transcendentals=0),
        name="mix",
    )(window, pos, p, l, own, near, far)


def rim(strips, frames):
    pairs = [(2 * j, 2 * j + 2) for j in range(frames - 1)] + [(2 * j + 3, 2 * j + 1) for j in range(frames - 1)]
    return lax.ppermute(strips, ("a", "core"), pairs)


def both(strips):
    return lax.all_gather(strips, "core")


def per_device(query_rows, key_rows, value_rows, window_offsets):
    frames, core = lax.axis_size("a"), lax.axis_index("core")
    pos = jnp.stack([lax.axis_index("a"), core]).astype(jnp.int32)
    by_column = [x.transpose(1, 0, 2) for x in (key_rows, value_rows, query_rows)]
    kvq = lax.all_to_all(pack(*by_column), ("i", "y"), 0, 0, tiled=True)
    k, v, q = kvq[:, 0], kvq[:, 1], kvq[:, 2]
    k_near = rim(k, frames)
    k_both = both(k)
    k_far = rim(lax.dynamic_index_in_dim(k_both, 1 - core, keepdims=False), frames)
    v_both = both(v)
    v_other = lax.dynamic_index_in_dim(v_both, 1 - core, keepdims=False)
    k_near, v, v_other = lax.optimization_barrier((k_near, v, v_other))
    v_near, v_far, k_near = rim(v, frames), rim(v_other, frames), both(k_near)
    k_near, k_far = lax.optimization_barrier((k_near, k_far))
    k_far = both(k_far)
    p, l = scores(window_offsets, pos, q, k_both, k_near, k_far, frames)
    p, v_near = lax.optimization_barrier((p, v_near))
    v_near = both(v_near)
    v_near, v_far = lax.optimization_barrier((v_near, v_far))
    out = mix(window_offsets, pos, p, l, v_both, v_near, both(v_far), frames)
    return unpack(lax.all_to_all(out, ("i", "y"), 0, 0, tiled=True)).transpose(1, 0, 2)


def solution(mesh):
    slabs, strips = mesh.devices.shape
    fine = Mesh(mesh.devices.reshape(slabs // 8, 8, strips // 2, 2), ("a", "i", "y", "core"))
    spec = P(("a", "i"), ("y", "core"), None)
    return jax.shard_map(
        per_device,
        mesh=fine,
        in_specs=(spec, spec, spec, P()),
        out_specs=spec,
        check_vma=False,
    )
```

```python
import jax
import jax.numpy as jnp
from jax import lax
from jax.experimental import pallas as pl
from jax.experimental.pallas import tpu as pltpu
from jax.sharding import Mesh, PartitionSpec as P

HD = 128
HEADS = 32
STRIP = 6
ROWS = 8
PIECE = STRIP * ROWS
SPAN = 8 * PIECE
CHUNK = 64
TILE = 256
COLS = 6
WIN = 8
CHIPS = 32
C2 = HD ** (-0.5) * 1.4426950408889634


def pack_body(*refs):
    count = len(refs) // 2 - 1
    ins, out_ref, held, sems = refs[:count], refs[count], refs[count + 1 : -1], refs[-1]
    copies = [pltpu.make_async_copy(ins[n], held[n], sems.at[n]) for n in range(count)]
    for copy in copies:
        copy.start()
    for n in range(count):
        copies[n].wait()
        for h in range(HEADS):
            piece = held[n][:, :, HD * h : HD * h + HD].astype(jnp.float32)
            out_ref[h, n] = piece.reshape(PIECE, HD).astype(jnp.bfloat16)


def pack(*arrays):
    count = len(arrays)
    arrays = [pltpu.with_memory_space_constraint(x, pltpu.HBM) for x in arrays]
    return pl.pallas_call(
        pack_body,
        out_shape=jax.ShapeDtypeStruct((HEADS, count, PIECE, HD), jnp.bfloat16),
        in_specs=[pl.BlockSpec(memory_space=pltpu.HBM)] * count,
        out_specs=pl.BlockSpec(memory_space=pltpu.VMEM),
        scratch_shapes=[pltpu.VMEM((STRIP, ROWS, HEADS * HD), jnp.bfloat16)] * count
        + [pltpu.SemaphoreType.DMA((count,))],
        compiler_params=pltpu.CompilerParams(vmem_limit_bytes=16 << 20),
        cost_estimate=pl.CostEstimate(flops=0, bytes_accessed=count * 800_000, transcendentals=0),
        name="pack",
    )(*arrays)


def unpack_body(in_ref, out_ref):
    for h in range(HEADS):
        piece = in_ref[h].astype(jnp.float32).reshape(STRIP, ROWS, HD)
        out_ref[:, :, HD * h : HD * h + HD] = piece.astype(jnp.bfloat16)


def unpack(array):
    return pl.pallas_call(
        unpack_body,
        out_shape=jax.ShapeDtypeStruct((STRIP, ROWS, HEADS * HD), jnp.bfloat16),
        compiler_params=pltpu.CompilerParams(vmem_limit_bytes=16 << 20),
        cost_estimate=pl.CostEstimate(flops=0, bytes_accessed=800_000, transcendentals=0),
        name="unpack",
    )(array)


def assemble(full, own_ref, near_ref, far_ref):
    def fill(i, carry):
        for ref, frame, swap in ((own_ref, 1, 0), (near_ref, None, 0), (far_ref, None, 1)):
            for c in range(2):
                for y in range(4):
                    p = 2 * y + (c ^ swap)
                    d = 2 * c if frame is None else frame
                    full[d, i, PIECE * p : PIECE * p + PIECE, :] = ref[c, i * 4 + y]
        return carry

    lax.fori_loop(0, 8, fill, 0)


def groups(step, core):
    b, half = step // 2, step % 2
    flip = 1 - core
    return b, half, (
        (3, 0, core, 0, 2 * core),
        (2, 192, flip, 16 * core, 1),
        (1, 320, flip, 32 * flip, 2 * flip),
    )


def key_tile(win_ref, frame, frames, b, c, w):
    dt, kb, kc = win_ref[w, 0], b + win_ref[w, 1], c + win_ref[w, 2]
    kt = frame + dt
    live = (kt >= 0) & (kt < frames) & (kb >= 0) & (kb < 2) & (kc >= 0) & (kc < COLS)
    return live, dt + 1, kb, kc


def tile_rows(full, d, kb, kc):
    start = pl.multiple_of(kc * CHUNK, CHUNK)
    return jnp.concatenate([full[d, 2 * f + kb, pl.ds(start, CHUNK), :] for f in range(4)], axis=0)


def score_body(frames, win_ref, pos_ref, q_ref, own_ref, near_ref, far_ref, p_ref, l_ref, keys, s_ref):
    frame, core = pos_ref[0], pos_ref[1]
    assemble(keys, own_ref, near_ref, far_ref)

    def step_body(step, carry):
        b, half, parts = groups(step, core)
        for size, base, j, first, t in parts:
            count = CHUNK * size
            c = 3 * half + t
            first = pl.multiple_of(first, 16)
            q = jnp.concatenate(
                [q_ref[(2 * f + b) * 4 + 2 * half + j, pl.ds(first, 16 * size), :] for f in range(4)], axis=0
            )
            most = None
            lives = []
            for w in range(WIN):
                live, d, kb, kc = key_tile(win_ref, frame, frames, b, c, w)
                lives.append(live)
                k = tile_rows(keys, jnp.where(live, d, 1), jnp.where(live, kb, b), jnp.where(live, kc, c))
                s = lax.dot_general(q, k, (((1,), (1,)), ((), ())), preferred_element_type=jnp.float32)
                s_ref[w, 0:count, :] = s
                high = jnp.maximum(s[:, :HD], s[:, HD:])
                most = high if most is None else jnp.maximum(most, high)
            top = jnp.max(most, axis=1, keepdims=True)
            total = jnp.zeros((count, HD), jnp.float32)
            for w in range(WIN):
                p = jnp.exp2((s_ref[w, 0:count, :] - top) * C2)
                total += jnp.where(lives[w], p[:, :HD] + p[:, HD:], 0.0)
                p_ref[step, base : base + count, TILE * w : TILE * w + TILE] = p.astype(jnp.bfloat16)
            total = jnp.sum(total, axis=1, keepdims=True)
            l_ref[step, base : base + count, :] = jnp.broadcast_to(1.0 / total, (count, HD))
        return carry

    for step in range(4):
        step_body(step, 0)


def mix_body(frames, win_ref, pos_ref, p_ref, l_ref, own_ref, near_ref, far_ref, out_ref, values):
    frame, core = pos_ref[0], pos_ref[1]
    assemble(values, own_ref, near_ref, far_ref)
    for f in range(4):
        values[3, 2 * f, 0:CHUNK, :] = jnp.zeros((CHUNK, HD), jnp.bfloat16)

    def step_body(step, carry):
        b, half, parts = groups(step, core)
        for size, base, j, first, t in parts:
            count = CHUNK * size
            c = 3 * half + t
            first = pl.multiple_of(first, 16)
            tiles = []
            for w in range(WIN):
                live, d, kb, kc = key_tile(win_ref, frame, frames, b, c, w)
                tiles.append(tile_rows(values, jnp.where(live, d, 3), jnp.where(live, kb, 0), jnp.where(live, kc, 0)))
            o = jnp.dot(
                p_ref[step, base : base + count, :], jnp.concatenate(tiles, axis=0), preferred_element_type=jnp.float32
            )
            o = (o * l_ref[step, base : base + count, :]).astype(jnp.bfloat16)
            for f in range(4):
                out_ref[(2 * f + b) * 4 + 2 * half + j, pl.ds(first, 16 * size), :] = o[
                    16 * size * f : 16 * size * (f + 1)
                ]
        return carry

    for step in range(4):
        step_body(step, 0)


SMALL = pl.BlockSpec(memory_space=pltpu.SMEM)
LOCAL = pl.BlockSpec(memory_space=pltpu.VMEM)


def scores(window, pos, q, own, near, far, frames):
    return pl.pallas_call(
        lambda *refs: score_body(frames, *refs),
        out_shape=(
            jax.ShapeDtypeStruct((4, 384, WIN * TILE), jnp.bfloat16),
            jax.ShapeDtypeStruct((4, 384, HD), jnp.float32),
        ),
        in_specs=[SMALL] * 2 + [LOCAL] * 4,
        out_specs=(LOCAL, LOCAL),
        scratch_shapes=[
            pltpu.VMEM((3, 8, SPAN, HD), jnp.bfloat16),
            pltpu.VMEM((WIN, 192, TILE), jnp.float32),
        ],
        compiler_params=pltpu.CompilerParams(vmem_limit_bytes=24 << 20),
        cost_estimate=pl.CostEstimate(flops=1_000_000, bytes_accessed=1_000_000, transcendentals=0),
        name="scores",
    )(window, pos, q, own, near, far)


def mix(window, pos, p, l, own, near, far, frames):
    return pl.pallas_call(
        lambda *refs: mix_body(frames, *refs),
        out_shape=jax.ShapeDtypeStruct((CHIPS, PIECE, HD), jnp.bfloat16),
        in_specs=[SMALL] * 2 + [LOCAL] * 5,
        out_specs=LOCAL,
        scratch_shapes=[pltpu.VMEM((4, 8, SPAN, HD), jnp.bfloat16)],
        compiler_params=pltpu.CompilerParams(vmem_limit_bytes=24 << 20),
        cost_estimate=pl.CostEstimate(flops=810_000_000, bytes_accessed=10_000_000, transcendentals=0),
        name="mix",
    )(window, pos, p, l, own, near, far)


def rim(strips, frames):
    pairs = [(2 * j, 2 * j + 2) for j in range(frames - 1)] + [(2 * j + 3, 2 * j + 1) for j in range(frames - 1)]
    return lax.ppermute(strips, ("a", "core"), pairs)


def both(strips):
    return lax.all_gather(strips, "core")


def per_device(query_rows, key_rows, value_rows, window_offsets):
    frames, core = lax.axis_size("a"), lax.axis_index("core")
    pos = jnp.stack([lax.axis_index("a"), core]).astype(jnp.int32)
    by_column = [x.transpose(1, 0, 2) for x in (key_rows, value_rows, query_rows)]
    kvq = lax.all_to_all(pack(*by_column), ("i", "y"), 0, 0, tiled=True)
    k, v, q = kvq[:, 0], kvq[:, 1], kvq[:, 2]
    k_near = rim(k, frames)
    k_both = both(k)
    k_far = rim(lax.dynamic_index_in_dim(k_both, 1 - core, keepdims=False), frames)
    v_both = both(v)
    v_other = lax.dynamic_index_in_dim(v_both, 1 - core, keepdims=False)
    k_near, v, v_other = lax.optimization_barrier((k_near, v, v_other))
    v_near, v_far, k_near = rim(v, frames), rim(v_other, frames), both(k_near)
    k_near, k_far = lax.optimization_barrier((k_near, k_far))
    k_far = both(k_far)
    p, l = scores(window_offsets, pos, q, k_both, k_near, k_far, frames)
    p, v_near = lax.optimization_barrier((p, v_near))
    v_near = both(v_near)
    v_near, v_far = lax.optimization_barrier((v_near, v_far))
    out = mix(window_offsets, pos, p, l, v_both, v_near, both(v_far), frames)
    return unpack(lax.all_to_all(out, ("i", "y"), 0, 0, tiled=True)).transpose(1, 0, 2)


def solution(mesh):
    slabs, strips = mesh.devices.shape
    fine = Mesh(mesh.devices.reshape(slabs // 8, 8, strips // 2, 2), ("a", "i", "y", "core"))
    spec = P(("a", "i"), ("y", "core"), None)
    return jax.shard_map(
        per_device,
        mesh=fine,
        in_specs=(spec, spec, spec, P()),
        out_specs=spec,
        check_vma=False,
    )
```

```python
import jax
import jax.numpy as jnp
from jax import lax
from jax.experimental import pallas as pl
from jax.experimental.pallas import tpu as pltpu
from jax.sharding import Mesh, PartitionSpec as P

HD = 128
HEADS = 32
STRIP = 6
ROWS = 8
PIECE = STRIP * ROWS
SPAN = 8 * PIECE
CHUNK = 64
TILE = 256
COLS = 6
WIN = 8
CHIPS = 32
C2 = HD ** (-0.5) * 1.4426950408889634


def pack_body(*refs):
    count = len(refs) // 2 - 1
    ins, out_ref, held, sems = refs[:count], refs[count], refs[count + 1 : -1], refs[-1]
    copies = [pltpu.make_async_copy(ins[n], held[n], sems.at[n]) for n in range(count)]
    for copy in copies:
        copy.start()
    for n in range(count):
        copies[n].wait()
        for h in range(HEADS):
            piece = held[n][:, :, HD * h : HD * h + HD].astype(jnp.float32)
            out_ref[h, n] = piece.reshape(PIECE, HD).astype(jnp.bfloat16)


def pack(*arrays):
    count = len(arrays)
    arrays = [pltpu.with_memory_space_constraint(x, pltpu.HBM) for x in arrays]
    return pl.pallas_call(
        pack_body,
        out_shape=jax.ShapeDtypeStruct((HEADS, count, PIECE, HD), jnp.bfloat16),
        in_specs=[pl.BlockSpec(memory_space=pltpu.HBM)] * count,
        out_specs=pl.BlockSpec(memory_space=pltpu.VMEM),
        scratch_shapes=[pltpu.VMEM((STRIP, ROWS, HEADS * HD), jnp.bfloat16)] * count
        + [pltpu.SemaphoreType.DMA((count,))],
        compiler_params=pltpu.CompilerParams(vmem_limit_bytes=16 << 20),
        cost_estimate=pl.CostEstimate(flops=0, bytes_accessed=count * 800_000, transcendentals=0),
        name="pack",
    )(*arrays)


def unpack_body(in_ref, out_ref, held, sems):
    part = HEADS // 4
    copies = []
    for g in range(4):
        for h in range(part * g, part * g + part):
            piece = in_ref[h].astype(jnp.float32).reshape(STRIP, ROWS, HD)
            held[g, :, :, HD * (h - part * g) : HD * (h - part * g) + HD] = piece.astype(jnp.bfloat16)
        lanes = pl.ds(HD * part * g, HD * part)
        copies.append(pltpu.make_async_copy(held.at[g], out_ref.at[:, :, lanes], sems.at[g]))
        copies[-1].start()
    for copy in copies:
        copy.wait()


def unpack(array):
    return pl.pallas_call(
        unpack_body,
        out_shape=jax.ShapeDtypeStruct((STRIP, ROWS, HEADS * HD), jnp.bfloat16),
        in_specs=[pl.BlockSpec(memory_space=pltpu.VMEM)],
        out_specs=pl.BlockSpec(memory_space=pltpu.HBM),
        scratch_shapes=[
            pltpu.VMEM((4, STRIP, ROWS, HEADS * HD // 4), jnp.bfloat16),
            pltpu.SemaphoreType.DMA((4,)),
        ],
        compiler_params=pltpu.CompilerParams(vmem_limit_bytes=16 << 20),
        cost_estimate=pl.CostEstimate(flops=0, bytes_accessed=800_000, transcendentals=0),
        name="unpack",
    )(array)


def assemble(full, own_ref, near_ref, far_ref):
    def fill(i, carry):
        for ref, frame, swap in ((own_ref, 1, 0), (near_ref, None, 0), (far_ref, None, 1)):
            for c in range(2):
                for y in range(4):
                    p = 2 * y + (c ^ swap)
                    d = 2 * c if frame is None else frame
                    full[d, i, PIECE * p : PIECE * p + PIECE, :] = ref[c, i * 4 + y]
        return carry

    lax.fori_loop(0, 8, fill, 0)


def groups(step, core):
    b, half = step // 2, step % 2
    flip = 1 - core
    return b, half, (
        (3, 0, core, 0, 2 * core),
        (2, 192, flip, 16 * core, 1),
        (1, 320, flip, 32 * flip, 2 * flip),
    )


def key_tile(win_ref, frame, frames, b, c, w):
    dt, kb, kc = win_ref[w, 0], b + win_ref[w, 1], c + win_ref[w, 2]
    kt = frame + dt
    live = (kt >= 0) & (kt < frames) & (kb >= 0) & (kb < 2) & (kc >= 0) & (kc < COLS)
    return live, dt + 1, kb, kc


def tile_rows(full, d, kb, kc):
    start = pl.multiple_of(kc * CHUNK, CHUNK)
    return jnp.concatenate([full[d, 2 * f + kb, pl.ds(start, CHUNK), :] for f in range(4)], axis=0)


def score_body(frames, win_ref, pos_ref, q_ref, own_ref, near_ref, far_ref, p_ref, l_ref, keys, s_ref):
    frame, core = pos_ref[0], pos_ref[1]
    assemble(keys, own_ref, near_ref, far_ref)

    def step_body(step, carry):
        b, half, parts = groups(step, core)
        for size, base, j, first, t in parts:
            count = CHUNK * size
            c = 3 * half + t
            first = pl.multiple_of(first, 16)
            q = jnp.concatenate(
                [q_ref[(2 * f + b) * 4 + 2 * half + j, pl.ds(first, 16 * size), :] for f in range(4)], axis=0
            )
            most = None
            lives = []
            for w in range(WIN):
                live, d, kb, kc = key_tile(win_ref, frame, frames, b, c, w)
                lives.append(live)
                k = tile_rows(keys, jnp.where(live, d, 1), jnp.where(live, kb, b), jnp.where(live, kc, c))
                s = lax.dot_general(q, k, (((1,), (1,)), ((), ())), preferred_element_type=jnp.float32)
                s_ref[w, 0:count, :] = s
                high = jnp.maximum(s[:, :HD], s[:, HD:])
                most = high if most is None else jnp.maximum(most, high)
            top = jnp.max(most, axis=1, keepdims=True)
            total = jnp.zeros((count, HD), jnp.float32)
            for w in range(WIN):
                p = jnp.exp2((s_ref[w, 0:count, :] - top) * C2)
                total += jnp.where(lives[w], p[:, :HD] + p[:, HD:], 0.0)
                p_ref[step, base : base + count, TILE * w : TILE * w + TILE] = p.astype(jnp.bfloat16)
            total = jnp.sum(total, axis=1, keepdims=True)
            l_ref[step, base : base + count, :] = jnp.broadcast_to(1.0 / total, (count, HD))
        return carry

    for step in range(4):
        step_body(step, 0)


def mix_body(frames, win_ref, pos_ref, p_ref, l_ref, own_ref, near_ref, far_ref, out_ref, values):
    frame, core = pos_ref[0], pos_ref[1]
    assemble(values, own_ref, near_ref, far_ref)
    for f in range(4):
        values[3, 2 * f, 0:CHUNK, :] = jnp.zeros((CHUNK, HD), jnp.bfloat16)

    def step_body(step, carry):
        b, half, parts = groups(step, core)
        for size, base, j, first, t in parts:
            count = CHUNK * size
            c = 3 * half + t
            first = pl.multiple_of(first, 16)
            tiles = []
            for w in range(WIN):
                live, d, kb, kc = key_tile(win_ref, frame, frames, b, c, w)
                tiles.append(tile_rows(values, jnp.where(live, d, 3), jnp.where(live, kb, 0), jnp.where(live, kc, 0)))
            o = jnp.dot(
                p_ref[step, base : base + count, :], jnp.concatenate(tiles, axis=0), preferred_element_type=jnp.float32
            )
            o = (o * l_ref[step, base : base + count, :]).astype(jnp.bfloat16)
            for f in range(4):
                out_ref[(2 * f + b) * 4 + 2 * half + j, pl.ds(first, 16 * size), :] = o[
                    16 * size * f : 16 * size * (f + 1)
                ]
        return carry

    for step in range(4):
        step_body(step, 0)


SMALL = pl.BlockSpec(memory_space=pltpu.SMEM)
LOCAL = pl.BlockSpec(memory_space=pltpu.VMEM)


def scores(window, pos, q, own, near, far, frames):
    return pl.pallas_call(
        lambda *refs: score_body(frames, *refs),
        out_shape=(
            jax.ShapeDtypeStruct((4, 384, WIN * TILE), jnp.bfloat16),
            jax.ShapeDtypeStruct((4, 384, HD), jnp.float32),
        ),
        in_specs=[SMALL] * 2 + [LOCAL] * 4,
        out_specs=(LOCAL, LOCAL),
        scratch_shapes=[
            pltpu.VMEM((3, 8, SPAN, HD), jnp.bfloat16),
            pltpu.VMEM((WIN, 192, TILE), jnp.float32),
        ],
        compiler_params=pltpu.CompilerParams(vmem_limit_bytes=24 << 20),
        cost_estimate=pl.CostEstimate(flops=1_000_000, bytes_accessed=1_000_000, transcendentals=0),
        name="scores",
    )(window, pos, q, own, near, far)


def mix(window, pos, p, l, own, near, far, frames):
    return pl.pallas_call(
        lambda *refs: mix_body(frames, *refs),
        out_shape=jax.ShapeDtypeStruct((CHIPS, PIECE, HD), jnp.bfloat16),
        in_specs=[SMALL] * 2 + [LOCAL] * 5,
        out_specs=LOCAL,
        scratch_shapes=[pltpu.VMEM((4, 8, SPAN, HD), jnp.bfloat16)],
        compiler_params=pltpu.CompilerParams(vmem_limit_bytes=24 << 20),
        cost_estimate=pl.CostEstimate(flops=810_000_000, bytes_accessed=10_000_000, transcendentals=0),
        name="mix",
    )(window, pos, p, l, own, near, far)


def rim(strips, frames):
    pairs = [(2 * j, 2 * j + 2) for j in range(frames - 1)] + [(2 * j + 3, 2 * j + 1) for j in range(frames - 1)]
    return lax.ppermute(strips, ("a", "core"), pairs)


def both(strips):
    return lax.all_gather(strips, "core")


def per_device(query_rows, key_rows, value_rows, window_offsets):
    frames, core = lax.axis_size("a"), lax.axis_index("core")
    pos = jnp.stack([lax.axis_index("a"), core]).astype(jnp.int32)
    by_column = [x.transpose(1, 0, 2) for x in (key_rows, value_rows, query_rows)]
    kvq = lax.all_to_all(pack(*by_column), ("i", "y"), 0, 0, tiled=True)
    k, v, q = kvq[:, 0], kvq[:, 1], kvq[:, 2]
    k_near = rim(k, frames)
    k_both = both(k)
    k_far = rim(lax.dynamic_index_in_dim(k_both, 1 - core, keepdims=False), frames)
    v_both = both(v)
    v_other = lax.dynamic_index_in_dim(v_both, 1 - core, keepdims=False)
    k_near, v, v_other = lax.optimization_barrier((k_near, v, v_other))
    v_near, v_far, k_near = rim(v, frames), rim(v_other, frames), both(k_near)
    k_near, k_far = lax.optimization_barrier((k_near, k_far))
    k_far = both(k_far)
    p, l = scores(window_offsets, pos, q, k_both, k_near, k_far, frames)
    p, v_near = lax.optimization_barrier((p, v_near))
    v_near = both(v_near)
    v_near, v_far = lax.optimization_barrier((v_near, v_far))
    out = mix(window_offsets, pos, p, l, v_both, v_near, both(v_far), frames)
    return unpack(lax.all_to_all(out, ("i", "y"), 0, 0, tiled=True)).transpose(1, 0, 2)


def solution(mesh):
    slabs, strips = mesh.devices.shape
    fine = Mesh(mesh.devices.reshape(slabs // 8, 8, strips // 2, 2), ("a", "i", "y", "core"))
    spec = P(("a", "i"), ("y", "core"), None)
    return jax.shard_map(
        per_device,
        mesh=fine,
        in_specs=(spec, spec, spec, P()),
        out_specs=spec,
        check_vma=False,
    )
```
